32 devices in a mesh: grp: 2 (over core), ep: 16 (over z, y, x).
Axes of the slice: x: 2, y: 2, z: 4, core: 2. Of those that a mesh axis runs over, the one named last changes fastest.
Arguments:
- out_grad: bfloat16 [16384, 2048], P(('grp', 'ep')), may hold values from -0.5 to 0.5
- probs: float32 [16384, 8], P(('grp', 'ep')), may hold values from 0.02 to 0.5
- dest: int32 [16384, 8], P(('grp', 'ep')), may hold values from -1 to 49151, as said below
- replica_owner: int32 [2, 16], P('grp'), may hold values from 0 to 15, as said below
- gate_up: bfloat16 [98304, 1536], P(('grp', 'ep')), may hold values from -6 to 6
Outputs:
- d_down: float32 [16, 768, 2048], P('ep', None, 'grp')
The draws below stay inside these ranges and needn't reach their ends.
Inputs may be any that keep to these rules, and one draw needn't show every extreme that they name: `dest`: copies of one token name distinct rows; a device's copies to slot buffer (j, s) fill the rows of that buffer's block for the device, which is the device's ep index times 96 onward, from its start without gaps; in every draw some device fills its block of some buffer, all 96 rows, and copies beyond a block are dropped. `replica_owner`: each entry names an expert that has its primary slot on that ep index of the group.
All inputs are finite; a program needn't handle non-finite values.
Results may differ from the reference program's by a relative error of at most 0.005.
Values may be sent and summed in bfloat16 or wider, within the bound.
A program may use at most 128 MiB of HBM per device.

```python
import math
import jax
import jax.numpy as jnp
from jax import lax

D = 2048
H = 768
TOP = 8
TOK_DEV = 512
EXPERTS = 16
HOT = 4
CAP = 1536
C_SRC = 96
TOKEN_TOTAL = 16384
SLOT_ROWS = 98304
N_GRP = 2
N_EP = 16


def plan_group(group_key):
    first, second_replica, third = jax.random.split(group_key, 3)
    experts = jnp.arange(EXPERTS, dtype=jnp.int32)
    order = jax.random.permutation(first, EXPERTS).astype(jnp.int32)
    hotness = jnp.zeros((EXPERTS,), jnp.int32).at[order[:HOT]].set(1)
    owners = order[jax.random.randint(second_replica, (EXPERTS,), 0, HOT)]
    bits = jax.random.randint(third, (EXPERTS * TOK_DEV, EXPERTS), 0, 1 << 20)
    score = bits * (1 + 2 * hotness)[None, :] * 64 + experts[None, :]
    unused, chosen_experts = lax.top_k(score, TOP)
    chosen_experts = chosen_experts.astype(jnp.int32).reshape(EXPERTS, TOK_DEV * TOP)
    onehot = (chosen_experts[:, :, None] == experts[None, None, :]).astype(jnp.int32)
    before = jnp.cumsum(onehot, axis=1) - onehot
    count = jnp.sum(before * onehot, axis=2)
    match_flags = (owners[None, :] == experts[:, None]).astype(jnp.int32)
    slot_count = 1 + jnp.sum(match_flags, axis=1)
    ranks = jnp.cumsum(match_flags, axis=1) * match_flags
    token_share = slot_count[chosen_experts]
    turn = count % token_share
    place = count // token_share
    picked = jnp.sum(experts[None, None, :] * (ranks[chosen_experts] == turn[:, :, None]).astype(jnp.int32), axis=2)
    device = jnp.where(turn == 0, chosen_experts, picked)
    second_slot = jnp.where(turn == 0, 0, 1)
    source = experts[:, None]
    target = device * 2 * CAP + second_slot * CAP + source * C_SRC + place
    target = jnp.where(place < C_SRC, target, -1)
    return (owners, target.reshape(EXPERTS * TOK_DEV, TOP))


def plan_all(key):
    base = jax.random.fold_in(key, 7)
    keys = jax.random.split(base, N_GRP)
    owners, targets = jax.vmap(plan_group)(keys)
    return (owners.astype(jnp.int32), targets.reshape(N_GRP * EXPERTS * TOK_DEV, TOP).astype(jnp.int32))


def draw_dest(key, part):
    owners, targets = plan_all(key)
    return targets


def draw_replica_owner(key, part):
    owners, targets = plan_all(key)
    return owners


def block_levels(stream_key, dims, pieces, low, top_value):
    def one(axis_at, shards_of):
        heights = jax.random.uniform(jax.random.fold_in(jax.random.fold_in(stream_key, 6), axis_at), (shards_of,), jnp.float32, low / len(pieces), top_value / len(pieces))
        return jnp.repeat(jnp.exp(heights), dims[axis_at] // shards_of).reshape((-1,) + (1,) * (len(dims) - axis_at - 1))

    level = one(*pieces[0])
    for cut in pieces[1:]:
        level = level * one(*cut)
    return level


def bell_draw(key, dims, spread, reach, cuts=(), kind=jnp.bfloat16):
    drawn = jax.random.normal(key, dims, jnp.float32) * spread
    if len(cuts) > 0:
        drawn = block_levels(key, dims, cuts, -0.22, 0.18) * drawn
    return jnp.clip(drawn, min=-reach, max=reach).astype(kind)


def setup_inputs(seed: int = 0) -> dict:
    arg_keys = jax.random.split(jax.random.key(seed), 6)
    out_grad = bell_draw(arg_keys[0], (TOKEN_TOTAL, D), 0.08, 0.5, ((0, 32),))
    probs = jnp.clip(jnp.exp(math.log(0.5) - 3.218876 * jax.random.uniform(arg_keys[1], (TOKEN_TOTAL, TOP), jnp.float32) ** block_levels(arg_keys[1], (TOKEN_TOTAL, TOP), ((0, 32),), -0.2, 0.2)), 0.02, 0.5)
    dest = draw_dest(jax.random.fold_in(arg_keys[5], 71), 0)
    replica_owner = draw_replica_owner(jax.random.fold_in(arg_keys[5], 71), 0)
    gate_up = bell_draw(arg_keys[4], (SLOT_ROWS, 2 * H), 1.0, 6.0, ((0, 32),))
    return {"out_grad": out_grad, "probs": probs, "dest": dest, "replica_owner": replica_owner, "gate_up": gate_up}


def reference(out_grad, probs, dest, replica_owner, gate_up):
    group_rows = 2 * N_EP * CAP
    group_tokens = N_EP * TOK_DEV
    total = jnp.zeros((N_EP, H, D), jnp.float32)
    for group in range(N_GRP):
        lower = group * group_tokens
        grad_rows = out_grad[lower:lower + group_tokens]
        flat_weights = probs[lower:lower + group_tokens].astype(jnp.float32).reshape(-1)
        targets = dest[lower:lower + group_tokens].astype(jnp.int32)
        index = jnp.where(targets >= 0, targets, group_rows).reshape(-1).astype(jnp.int32)
        copy_of = jnp.full((group_rows,), -1, jnp.int32).at[index].set(
            jnp.arange(group_tokens * TOP, dtype=jnp.int32), mode="drop")
        owners = replica_owner[group].astype(jnp.int32)
        row_start = group * group_rows

        def per_device(device, carry):
            device = jnp.asarray(device).astype(jnp.int32)
            base = (device * 2 * CAP).astype(jnp.int32)
            rows = lax.dynamic_slice_in_dim(copy_of, base, 2 * CAP, 0)
            safe = jnp.maximum(rows, 0).astype(jnp.int32)
            weight = jnp.where(rows >= 0, flat_weights[safe], jnp.zeros_like(flat_weights[safe]))
            picked = grad_rows[(safe // TOP).astype(jnp.int32)].astype(jnp.float32)
            grads = (weight[:, None] * picked).astype(jnp.bfloat16)
            saved = lax.dynamic_slice_in_dim(gate_up, (base + row_start).astype(jnp.int32), 2 * CAP, 0)
            act = (jax.nn.silu(saved[:, :H].astype(jnp.float32)) * saved[:, H:].astype(jnp.float32)).astype(jnp.bfloat16)
            tile_main = jnp.dot(act[:CAP].T, grads[:CAP], preferred_element_type=jnp.float32).astype(jnp.bfloat16)
            tile_copy = jnp.dot(act[CAP:].T, grads[CAP:], preferred_element_type=jnp.float32).astype(jnp.bfloat16)
            tile_main, tile_copy = lax.optimization_barrier((tile_main, tile_copy))
            carry = carry.at[device].add(tile_main.astype(jnp.float32))
            carry = carry.at[owners[device]].add(tile_copy.astype(jnp.float32))
            return carry

        total = lax.fori_loop(0, N_EP, per_device, total)
    return total
```

```python
import functools

import jax
import jax.numpy as jnp
from jax import lax
from jax.experimental import pallas as pl
from jax.experimental.pallas import tpu as pltpu
from jax.sharding import PartitionSpec as P

MESH = pl.DeviceIdType.MESH
LINE = 4
MAX_CHUNKS = 8
ACT_ROWS = 128
AHEAD = 2
REP_LAG = 2
SUM_ROWS = 32


def dispatch_kernel(
    n_ep, n_grp, per_src, top, chunks,
    owners, meta_hbm, og_hbm, gu_hbm, out_ref,
    tok, metas, ownv, sel, outb, inb, act_t, gubuf,
    tiles, mine, pieces, zbuf, back,
    ld_sem, gu_sem, own_send, own_recv, zsend, zrecv, gsend, grecv,
    asend, arecv, bsend, brecv, bown, csend, crecv, dsend, drecv,
):
    n_in = n_ep // LINE
    g = lax.axis_index("grp")
    e = lax.axis_index("ep")
    z = e // n_in
    p = e % n_in
    cols = tok.shape[3]
    share = mine.shape[3]
    tokens = tok.shape[2]
    hidden = act_t.shape[1]
    cap = act_t.shape[2]
    hq = hidden // n_in
    near = n_in * n_grp
    block = 2 * per_src
    share_cols = pl.ds(pl.multiple_of(g * share, 128), share)

    m = ((z + 1) // 2) % 2
    far, rev = (z + 2) % 4, 3 - z
    order = [z, z + 1 - 2 * (z % 2), (1 - m) * far + m * rev, (1 - m) * rev + m * far]

    def wait_bytes(ref, sem):
        pltpu.make_async_copy(ref, ref, sem).wait()

    def load(c, part):
        return pltpu.make_async_copy(
            og_hbm.at[:, pl.ds(pl.multiple_of((part * chunks + c) * share, 128), share)],
            tok.at[c, z, :, pl.ds(part * share, share)], ld_sem.at[c, part])

    def load_meta():
        return pltpu.make_async_copy(meta_hbm, metas.at[z], ld_sem.at[chunks, 0])

    def gu_load(q, slot):
        return pltpu.make_async_copy(
            gu_hbm.at[pl.ds(pl.multiple_of(q * ACT_ROWS, ACT_ROWS), ACT_ROWS), :], gubuf.at[slot], gu_sem.at[slot])

    act_blocks = cap // ACT_ROWS

    def gu_block(n):
        return lax.rem(n + act_blocks, 2 * act_blocks)

    load_meta().start()
    for c in range(chunks):
        for part in range(n_grp):
            load(c, part).start()
    gu_load(gu_block(0), 0).start()
    for j in range(n_ep):
        ownv[g, j] = jnp.full((8, 128), owners[0, j], jnp.int32).astype(jnp.float32)

    barrier = pltpu.get_barrier_semaphore()

    def close(q):
        return {"grp": lax.rem(g + q // n_in, n_grp), "ep": z * n_in + lax.rem(p + q % n_in, n_in)}

    def greet(q, carry):
        pl.semaphore_signal(barrier, inc=1, device_id=close(q), device_id_type=MESH)
        return carry

    lax.fori_loop(1, near, greet, 0)

    @pl.when(z > 0)
    def _():
        pl.semaphore_signal(barrier, inc=1, device_id={"ep": e - n_in}, device_id_type=MESH)

    @pl.when(z < LINE - 1)
    def _():
        pl.semaphore_signal(barrier, inc=1, device_id={"ep": e + n_in}, device_id_type=MESH)

    ends = jnp.where(z == 0, 1, 0) + jnp.where(z == LINE - 1, 1, 0)
    pl.semaphore_wait(barrier, near - 1 + 2 - ends)

    def own_copy(d):
        return pltpu.make_async_remote_copy(
            src_ref=ownv.at[g], dst_ref=ownv.at[g], send_sem=own_send.at[d - 1], recv_sem=own_recv.at[d - 1],
            device_id={"grp": lax.rem(g + d, n_grp)}, device_id_type=MESH)

    def zcopy(c, zd, way):
        ref = tok.at[c, zd]
        return pltpu.make_async_remote_copy(
            src_ref=ref, dst_ref=ref, send_sem=zsend.at[way, c, zd], recv_sem=zrecv.at[c, zd],
            device_id={"ep": e + (n_in if way else -n_in)}, device_id_type=MESH)

    def mcopy(zd, way):
        ref = metas.at[zd]
        return pltpu.make_async_remote_copy(
            src_ref=ref, dst_ref=ref, send_sem=zsend.at[way, chunks, zd], recv_sem=zrecv.at[chunks, zd],
            device_id={"ep": e + (n_in if way else -n_in)}, device_id_type=MESH)

    def each_hop(copy, zd, act):
        @pl.when((zd <= z) & (z < LINE - 1))
        def _():
            act(copy(1))

        @pl.when((zd >= z) & (z > 0))
        def _():
            act(copy(0))

    def own_z(c):
        for part in range(n_grp):
            load(c, part).wait()
        each_hop(lambda way: zcopy(c, z, way), z, lambda copy: copy.start())

    def arrive(c, i):
        zd = order[i]
        zcopy(c, zd, 0).wait_recv()
        each_hop(lambda way: zcopy(c, zd, way), zd, lambda copy: copy.start())

    def arrive_meta(i):
        zd = order[i]
        mcopy(zd, 0).wait_recv()
        each_hop(lambda way: mcopy(zd, way), zd, lambda copy: copy.start())

    def build_sel(i):
        zd = order[i]

        def body(d, carry):
            pp = lax.rem(p + d, n_in)
            for s in range(2):
                first = ((z * n_in + pp) * block + s * per_src).astype(jnp.float32)
                ids = lax.broadcasted_iota(jnp.int32, (per_src, tokens), 0).astype(jnp.float32) + first
                weights = jnp.zeros((per_src, tokens), jnp.float32)
                for k in range(top):
                    code = metas[zd, k:k + 1, :]
                    prob = metas[zd, top + k:top + k + 1, :]
                    weights = jnp.where(ids == code, prob, weights)
                sel[zd, s, pl.ds(pl.multiple_of(d * per_src, 16), per_src), :] = weights.astype(jnp.bfloat16)
            return carry

        lax.fori_loop(0, n_in, body, 0)

    def gcopy(c, i, s, d):
        src = order[i] * n_in + p
        return pltpu.make_async_remote_copy(
            src_ref=outb.at[c, i, s, d - 1],
            dst_ref=inb.at[c, s, pl.ds(pl.multiple_of(src * per_src, 16), per_src), :],
            send_sem=gsend.at[c], recv_sem=grecv.at[c, s],
            device_id={"ep": z * n_in + lax.rem(p + d, n_in)}, device_id_type=MESH)

    def pick(c, i, s):
        zd = order[i]
        picked = jnp.dot(sel[zd, s], tok[c, zd], preferred_element_type=jnp.float32).astype(jnp.bfloat16)
        for d in range(1, n_in):
            outb[c, i, s, d - 1] = picked[d * per_src:(d + 1) * per_src]
            gcopy(c, i, s, d).start()
        own = pl.ds(pl.multiple_of((zd * n_in + p) * per_src, 16), per_src)
        inb[c, s, own, :] = picked[:per_src]

    def make_act(first, count):
        def body(n, carry):
            slot = n % 2
            q = gu_block(n)
            gu_load(q, slot).wait()

            @pl.when(n + 1 < 2 * act_blocks)
            def _():
                gu_load(gu_block(n + 1), 1 - slot).start()

            gate = gubuf[slot, :, :hidden].astype(jnp.float32)
            up = gubuf[slot, :, hidden:].astype(jnp.float32)
            half = 0.5 * gate
            act = ((half + half * jnp.tanh(half)) * up).astype(jnp.bfloat16)
            s = q // act_blocks
            r = q % act_blocks
            act_t[s, :, pl.ds(pl.multiple_of(r * ACT_ROWS, ACT_ROWS), ACT_ROWS)] = act.T
            return carry

        lax.fori_loop(first, first + count, body, 0)

    def multiply(c, s):
        wait_bytes(inb.at[c, s, pl.ds(0, (n_ep - LINE) * per_src), :], grecv.at[c, s])
        rows_at = hidden // 2 if cols <= 256 else hidden // 4

        def body(r, carry):
            rows = pl.ds(pl.multiple_of(r * rows_at, 16), rows_at)
            tiles[c, s, rows, :] = jnp.dot(
                act_t[s, rows, :], inb[c, s], preferred_element_type=jnp.float32).astype(jnp.bfloat16)
            return carry

        lax.fori_loop(0, hidden // rows_at, body, 0)

    def swap(c, d):
        there = lax.rem(g + d, n_grp)
        return pltpu.make_async_remote_copy(
            src_ref=tiles.at[c, 0, :, pl.ds(pl.multiple_of(there * share, 128), share)],
            dst_ref=mine.at[c, d - 1],
            send_sem=asend.at[c], recv_sem=arecv.at[c],
            device_id={"grp": there}, device_id_type=MESH)

    def piece_src(c, q):
        there = close(q)
        row = lax.rem(p + q % n_in, n_in)
        return tiles.at[c, 1, pl.ds(pl.multiple_of(row * hq, 16), hq),
                        pl.ds(pl.multiple_of(there["grp"] * share, 128), share)]

    def spread(c, q):
        return pltpu.make_async_remote_copy(
            src_ref=piece_src(c, q), dst_ref=pieces.at[c, g * n_in + p],
            send_sem=bsend.at[c], recv_sem=brecv.at[c], device_id=close(q), device_id_type=MESH)

    def spread_own(c):
        return pltpu.make_async_copy(piece_src(c, 0), pieces.at[c, g * n_in + p], bown.at[c])

    def replica(c):
        multiply(c, 1)

        def body(q, carry):
            spread(c, q).start()
            return carry

        lax.fori_loop(1, near, body, 0)
        spread_own(c).start()

    def primary(c):
        multiply(c, 0)
        for d in range(1, n_grp):
            swap(c, d).start()

    def add_up(c, ze, extra, store):
        def rows_body(r, carry):
            rows = pl.ds(pl.multiple_of((r % (hq // SUM_ROWS)) * SUM_ROWS, 16), SUM_ROWS)
            lanes = pl.ds(pl.multiple_of((r // (hq // SUM_ROWS)) * 128, 128), 128)

            def add(gd, totals):
                for pk in range(n_in):
                    owner = ownv[gd, z * n_in + pk]
                    piece = pieces[c, gd * n_in + pk, rows, lanes].astype(jnp.float32)
                    piece = piece.reshape(SUM_ROWS // 8, 8, 128)
                    totals = tuple(
                        total + jnp.where((owner == (ze * n_in + b).astype(jnp.float32))[None], piece, 0.0)
                        for b, total in enumerate(totals))
                return totals

            zero = jnp.zeros((SUM_ROWS // 8, 8, 128), jnp.float32)
            totals = lax.fori_loop(0, n_grp, add, (zero,) * n_in)
            for b in range(n_in):
                store(b, rows, lanes, totals[b].reshape(SUM_ROWS, 128))
            return carry

        lax.fori_loop(0, (hq // SUM_ROWS) * (share // 128), rows_body, 0)

    def chain(c, ze, src, dst, way):
        return pltpu.make_async_remote_copy(
            src_ref=zbuf.at[c, src], dst_ref=zbuf.at[c, dst], send_sem=csend.at[c], recv_sem=crecv.at[c, dst],
            device_id={"ep": e + (n_in if way else -n_in)}, device_id_type=MESH)

    def chain_to(ze):
        return jnp.where(ze == z - 1, LINE, ze)

    def pass_on(c, ze):
        edge = (z == 0) | (z == LINE - 1)

        def put(b, rows, lanes, total):
            zbuf[c, ze, b, rows, lanes] = total.astype(jnp.bfloat16)

        def put_add(b, rows, lanes, total):
            total += zbuf[c, ze, b, rows, lanes].astype(jnp.float32)
            zbuf[c, ze, b, rows, lanes] = total.astype(jnp.bfloat16)

        @pl.when(edge)
        def _():
            add_up(c, ze, (), put)

        @pl.when(jnp.logical_not(edge))
        def _():
            chain(c, ze, ze, ze, 0).wait_recv()
            add_up(c, ze, (), put_add)

        @pl.when(ze > z)
        def _():
            chain(c, ze, ze, ze, 1).start()

        @pl.when(ze < z)
        def _():
            chain(c, ze, ze, chain_to(ze), 0).start()

    def sum_first(c):
        wait_bytes(pieces.at[c, pl.ds(0, near - 1)], brecv.at[c])
        spread_own(c).wait()
        pass_on(c, jnp.where(z < 2, LINE - 1, 0))
        pass_on(c, jnp.where(z < 2, 2, 1))

    def sum_second(c):
        pass_on(c, z + 1 - 2 * (z % 2))

    def give(c, d):
        there = lax.rem(p + d, n_in)
        return pltpu.make_async_remote_copy(
            src_ref=zbuf.at[c, z, there], dst_ref=back.at[c, p],
            send_sem=dsend.at[c], recv_sem=drecv.at[c],
            device_id={"ep": z * n_in + there}, device_id_type=MESH)

    def sum_last(c):
        def put(slots):
            def store(b, rows, lanes, total):
                for slot in slots:
                    total += zbuf[c, slot, b, rows, lanes].astype(jnp.float32)
                zbuf[c, z, b, rows, lanes] = total.astype(jnp.bfloat16)
            return store

        @pl.when(z > 0)
        def _():
            chain(c, z, z, z, 1).wait_recv()

        @pl.when(z < LINE - 1)
        def _():
            chain(c, z, z, LINE, 0).wait_recv()

        @pl.when(z == 0)
        def _():
            add_up(c, z, (), put((LINE,)))

        @pl.when(z == LINE - 1)
        def _():
            add_up(c, z, (), put((LINE - 1,)))

        @pl.when((z > 0) & (z < LINE - 1))
        def _():
            add_up(c, z, (), put((z, LINE)))

        for d in range(1, n_in):
            give(c, d).start()
        back[c, p] = zbuf[c, z, p]

    def finish(c):
        wait_bytes(mine.at[c], arecv.at[c])
        wait_bytes(back.at[c, pl.ds(0, n_in - 1)], drecv.at[c])
        lanes = pl.ds(pl.multiple_of(c * share, 128), share)

        def body(r, carry):
            rows = pl.ds(pl.multiple_of(r * hq, 16), hq)
            total = tiles[c, 0, rows, share_cols].astype(jnp.float32)
            for d in range(1, n_grp):
                total += mine[c, d - 1, rows, :].astype(jnp.float32)
            out_ref[rows, lanes] = total + back[c, r].astype(jnp.float32)
            return carry

        lax.fori_loop(0, n_in, body, 0)

    def drain(c):
        for i in range(LINE):
            zd = order[i]
            each_hop(lambda way: zcopy(c, zd, way), zd, lambda copy: copy.wait_send())
        wait_bytes(outb.at[c], gsend.at[c])
        wait_bytes(mine.at[c], asend.at[c])
        wait_bytes(pieces.at[c, pl.ds(0, near - 1)], bsend.at[c])
        wait_bytes(zbuf.at[c, pl.ds(0, LINE - 1)], csend.at[c])
        wait_bytes(back.at[c, pl.ds(0, n_in - 1)], dsend.at[c])

    load_meta().wait()
    each_hop(lambda way: mcopy(z, way), z, lambda copy: copy.start())
    for c in range(min(AHEAD, chunks)):
        own_z(c)
    for d in range(1, n_grp):
        own_copy(d).start()
    build_sel(0)
    pick(0, 0, 1)

    def at(t, lag, fn):
        @pl.when((t >= lag) & (t < chunks + lag))
        def _():
            fn(t - lag)

    per_step = act_blocks // LINE

    def iteration(t, carry):
        at(t, -AHEAD, own_z)
        for i in range(LINE):
            if i > 0:
                @pl.when(t == 0)
                def _():
                    arrive_meta(i)

                at(t, 0, lambda c: arrive(c, i))

                @pl.when(t == 0)
                def _():
                    build_sel(i)

            at(t, 0 if i else -1, lambda c: pick(c, i, 1))
            at(t, 1 if i else 0, lambda c: pick(c, i, 0))

            @pl.when(t < 2)
            def _():
                make_act(t * act_blocks + i * per_step, per_step)

            if i == 0:
                at(t, REP_LAG, replica)
            if i == 1:
                at(t, REP_LAG + 1, primary)
            if i == 2:
                at(t, REP_LAG + 1, sum_first)
            if i == 3:
                at(t, REP_LAG + 1, sum_second)
                at(t, REP_LAG + 2, sum_last)
                at(t, REP_LAG + 3, finish)
                at(t, REP_LAG + 4, drain)

        @pl.when(t == REP_LAG)
        def _():
            for d in range(1, n_grp):
                own_copy(d).wait()

        return carry

    lax.fori_loop(0, chunks + REP_LAG + 5, iteration, 0)
    for i in range(LINE):
        zd = order[i]
        each_hop(lambda way: mcopy(zd, way), zd, lambda copy: copy.wait_send())


def run_kernel(owners, meta, out_grad, gate_up, n_ep, n_grp, top):
    tokens, width = out_grad.shape
    cap = gate_up.shape[0] // 2
    hidden = gate_up.shape[1] // 2
    per_src = cap // n_ep
    n_in = n_ep // LINE
    chunks = max(1, min(MAX_CHUNKS, width // n_grp // 128))
    cols = width // chunks
    share = cols // n_grp
    hq = hidden // n_in
    near = n_in * n_grp
    bf16 = jnp.bfloat16
    dma = pltpu.SemaphoreType.DMA
    return pl.pallas_call(
        functools.partial(dispatch_kernel, n_ep, n_grp, per_src, top, chunks),
        out_shape=jax.ShapeDtypeStruct((hidden, width // n_grp), jnp.float32),
        in_specs=[pl.BlockSpec(memory_space=pltpu.SMEM)] + [pl.BlockSpec(memory_space=pl.ANY)] * 3,
        out_specs=pl.BlockSpec(memory_space=pltpu.VMEM),
        scratch_shapes=[
            pltpu.VMEM((chunks, LINE, tokens, cols), bf16),
            pltpu.VMEM((LINE, 2 * top, tokens), jnp.float32),
            pltpu.VMEM((n_grp, n_ep, 8, 128), jnp.float32),
            pltpu.VMEM((LINE, 2, n_in * per_src, tokens), bf16),
            pltpu.VMEM((chunks, LINE, 2, n_in - 1, per_src, cols), bf16),
            pltpu.VMEM((chunks, 2, cap, cols), bf16),
            pltpu.VMEM((2, hidden, cap), bf16),
            pltpu.VMEM((2, ACT_ROWS, 2 * hidden), bf16),
            pltpu.VMEM((chunks, 2, hidden, cols), bf16),
            pltpu.VMEM((chunks, n_grp - 1, hidden, share), bf16),
            pltpu.VMEM((chunks, near, hq, share), bf16),
            pltpu.VMEM((chunks, LINE + 1, n_in, hq, share), bf16),
            pltpu.VMEM((chunks, n_in, hq, share), bf16),
            dma((chunks + 1, n_grp)),
            dma((2,)),
            dma((n_grp - 1,)),
            dma((n_grp - 1,)),
            dma((2, chunks + 1, LINE)),
            dma((chunks + 1, LINE)),
            dma((chunks,)),
            dma((chunks, 2)),
            dma((chunks,)),
            dma((chunks,)),
            dma((chunks,)),
            dma((chunks,)),
            dma((chunks,)),
            dma((chunks,)),
            dma((chunks, LINE + 1)),
            dma((chunks,)),
            dma((chunks,)),
        ],
        compiler_params=pltpu.CompilerParams(
            collective_id=0, has_side_effects=True, vmem_limit_bytes=67043328),
    )(owners, meta, out_grad, gate_up)


def on_device(out_grad, probs, dest, replica_owner, gate_up):
    n_ep = lax.axis_size("ep")
    n_grp = lax.axis_size("grp")
    top = probs.shape[1]
    cap = gate_up.shape[0] // 2
    hidden = gate_up.shape[1] // 2
    per_src = cap // n_ep
    code = (dest // cap) * per_src + dest % per_src
    code = jnp.where(dest >= 0, code, -1)
    meta = jnp.concatenate([code.T.astype(jnp.float32), probs.T], axis=0)
    total = run_kernel(replica_owner, meta, out_grad, gate_up, n_ep, n_grp, top)
    return total.reshape(1, hidden, -1)


def solution(mesh):
    in_specs = (
        P(("grp", "ep"), None),
        P(("grp", "ep"), None),
        P(("grp", "ep"), None),
        P("grp", None),
        P(("grp", "ep"), None),
    )
    out_specs = P("ep", None, "grp")
    return jax.shard_map(
        on_device, mesh=mesh, in_specs=in_specs, out_specs=out_specs, check_vma=False
    )
```

```python
import functools

import jax
import jax.numpy as jnp
from jax import lax
from jax.experimental import pallas as pl
from jax.experimental.pallas import tpu as pltpu
from jax.sharding import PartitionSpec as P

MESH = pl.DeviceIdType.MESH
LINE = 4
MAX_CHUNKS = 8
ACT_ROWS = 128
AHEAD = 1
REP_LAG = 1
OWN_AHEAD = 4
PRI_LAG = 3
SUM_ROWS = 32


def dispatch_kernel(
    n_ep, n_grp, per_src, top, chunks,
    owners, meta_hbm, og_hbm, gu_hbm, out_ref,
    tok, metas, ownv, sel, wgt, outb, inb, act_t, gubuf,
    tiles, mine, pieces, zbuf, back,
    ld_sem, gu_sem, own_send, own_recv, zsend, zrecv, gsend, grecv,
    asend, arecv, bsend, brecv, bown, csend, crecv, dsend, drecv,
):
    n_in = n_ep // LINE
    g = lax.axis_index("grp")
    e = lax.axis_index("ep")
    z = e // n_in
    p = e % n_in
    cols = tok.shape[3]
    share = mine.shape[3]
    tokens = tok.shape[2]
    hidden = act_t.shape[1]
    cap = act_t.shape[2]
    hq = hidden // n_in
    near = n_in * n_grp
    block = 2 * per_src
    share_cols = pl.ds(pl.multiple_of(g * share, 128), share)

    m = ((z + 1) // 2) % 2
    far, rev = (z + 2) % 4, 3 - z
    order = [z, z + 1 - 2 * (z % 2), (1 - m) * far + m * rev, (1 - m) * rev + m * far]

    def wait_bytes(ref, sem):
        pltpu.make_async_copy(ref, ref, sem).wait()

    def load(c, part):
        return pltpu.make_async_copy(
            og_hbm.at[:, pl.ds(pl.multiple_of((part * chunks + c) * share, 128), share)],
            tok.at[c, z, :, pl.ds(part * share, share)], ld_sem.at[c, part])

    def load_meta():
        return pltpu.make_async_copy(meta_hbm, metas.at[z], ld_sem.at[chunks, 0])

    def gu_load(q, slot):
        return pltpu.make_async_copy(
            gu_hbm.at[pl.ds(pl.multiple_of(q * ACT_ROWS, ACT_ROWS), ACT_ROWS), :], gubuf.at[slot], gu_sem.at[slot])

    act_blocks = cap // ACT_ROWS

    def gu_block(n):
        return lax.rem(n + act_blocks, 2 * act_blocks)

    load_meta().start()
    for c in range(chunks):
        for part in range(n_grp):
            load(c, part).start()
    gu_load(gu_block(0), 0).start()
    for j in range(n_ep):
        ownv[g, j] = jnp.full((8, 128), owners[0, j], jnp.int32).astype(jnp.float32)

    barrier = pltpu.get_barrier_semaphore()

    def close(q):
        return {"grp": lax.rem(g + q // n_in, n_grp), "ep": z * n_in + lax.rem(p + q % n_in, n_in)}

    def greet(q, carry):
        pl.semaphore_signal(barrier, inc=1, device_id=close(q), device_id_type=MESH)
        return carry

    lax.fori_loop(1, near, greet, 0)

    @pl.when(z > 0)
    def _():
        pl.semaphore_signal(barrier, inc=1, device_id={"ep": e - n_in}, device_id_type=MESH)

    @pl.when(z < LINE - 1)
    def _():
        pl.semaphore_signal(barrier, inc=1, device_id={"ep": e + n_in}, device_id_type=MESH)

    ends = jnp.where(z == 0, 1, 0) + jnp.where(z == LINE - 1, 1, 0)
    pl.semaphore_wait(barrier, near - 1 + 2 - ends)

    def own_copy(d):
        return pltpu.make_async_remote_copy(
            src_ref=ownv.at[g], dst_ref=ownv.at[g], send_sem=own_send.at[d - 1], recv_sem=own_recv.at[d - 1],
            device_id={"grp": lax.rem(g + d, n_grp)}, device_id_type=MESH)

    def zcopy(c, zd, way):
        ref = tok.at[c, zd]
        return pltpu.make_async_remote_copy(
            src_ref=ref, dst_ref=ref, send_sem=zsend.at[way, c, zd], recv_sem=zrecv.at[c, zd],
            device_id={"ep": e + (n_in if way else -n_in)}, device_id_type=MESH)

    def mcopy(zd, way):
        ref = metas.at[zd]
        return pltpu.make_async_remote_copy(
            src_ref=ref, dst_ref=ref, send_sem=zsend.at[way, chunks, zd], recv_sem=zrecv.at[chunks, zd],
            device_id={"ep": e + (n_in if way else -n_in)}, device_id_type=MESH)

    def each_hop(copy, zd, act):
        @pl.when((zd <= z) & (z < LINE - 1))
        def _():
            act(copy(1))

        @pl.when((zd >= z) & (z > 0))
        def _():
            act(copy(0))

    def own_z(c):
        each_hop(lambda way: zcopy(c, z, way), z, lambda copy: copy.start())

    def arrive(c, i):
        zd = order[i]
        zcopy(c, zd, 0).wait_recv()
        each_hop(lambda way: zcopy(c, zd, way), zd, lambda copy: copy.start())

    def arrive_meta(i):
        zd = order[i]
        mcopy(zd, 0).wait_recv()
        each_hop(lambda way: mcopy(zd, way), zd, lambda copy: copy.start())

    def build_sel(i):
        zd = order[i]

        def body(d, carry):
            pp = lax.rem(p + d, n_in)
            for s in range(2):
                first = ((z * n_in + pp) * block + s * per_src).astype(jnp.float32)
                ids = lax.broadcasted_iota(jnp.int32, (per_src, tokens), 0).astype(jnp.float32) + first
                weights = jnp.zeros((per_src, tokens), jnp.float32)
                for k in range(top):
                    code = metas[zd, k:k + 1, :]
                    prob = metas[zd, top + k:top + k + 1, :]
                    weights = jnp.where(ids == code, prob, weights)
                rows = pl.ds(pl.multiple_of(d * per_src, 16), per_src)
                sel[zd, s, rows, :] = jnp.where(weights != 0.0, 1.0, 0.0).astype(jnp.bfloat16)
                wgt[zd, s, rows, :] = jnp.broadcast_to(
                    jnp.sum(weights, axis=1, keepdims=True), (per_src, wgt.shape[3]))
            return carry

        lax.fori_loop(0, n_in, body, 0)

    def gcopy(c, i, s, d):
        src = order[i] * n_in + p
        return pltpu.make_async_remote_copy(
            src_ref=outb.at[c, i, s, d - 1],
            dst_ref=inb.at[c, s, pl.ds(pl.multiple_of(src * per_src, 16), per_src), :],
            send_sem=gsend.at[c], recv_sem=grecv.at[c, s],
            device_id={"ep": z * n_in + lax.rem(p + d, n_in)}, device_id_type=MESH)

    def pick(c, i, s):
        zd = order[i]
        picked = jnp.dot(sel[zd, s], tok[c, zd], preferred_element_type=jnp.float32)
        picked = (picked * jnp.tile(wgt[zd, s], (1, cols // 128))).astype(jnp.bfloat16)
        for d in range(1, n_in):
            outb[c, i, s, d - 1] = picked[d * per_src:(d + 1) * per_src]
            gcopy(c, i, s, d).start()
        own = pl.ds(pl.multiple_of((zd * n_in + p) * per_src, 16), per_src)
        inb[c, s, own, :] = picked[:per_src]

    def make_act(first, count):
        def body(n, carry):
            slot = n % 2
            q = gu_block(n)
            gu_load(q, slot).wait()

            @pl.when(n + 1 < 2 * act_blocks)
            def _():
                gu_load(gu_block(n + 1), 1 - slot).start()

            gate = gubuf[slot, :, :hidden].astype(jnp.float32)
            up = gubuf[slot, :, hidden:].astype(jnp.float32)
            half = 0.5 * gate
            act = ((half + half * jnp.tanh(half)) * up).astype(jnp.bfloat16)
            s = q // act_blocks
            r = q % act_blocks
            act_t[s, :, pl.ds(pl.multiple_of(r * ACT_ROWS, ACT_ROWS), ACT_ROWS)] = act.T
            return carry

        lax.fori_loop(first, first + count, body, 0)

    def multiply(c, s):
        wait_bytes(inb.at[c, s, pl.ds(0, (n_ep - LINE) * per_src), :], grecv.at[c, s])
        rows_at = hidden // 2 if cols <= 256 else hidden // 4

        def body(r, carry):
            rows = pl.ds(pl.multiple_of(r * rows_at, 16), rows_at)
            tiles[c, s, rows, :] = jnp.dot(
                act_t[s, rows, :], inb[c, s], preferred_element_type=jnp.float32).astype(jnp.bfloat16)
            return carry

        lax.fori_loop(0, hidden // rows_at, body, 0)

    def swap(c, d):
        there = lax.rem(g + d, n_grp)
        return pltpu.make_async_remote_copy(
            src_ref=tiles.at[c, 0, :, pl.ds(pl.multiple_of(there * share, 128), share)],
            dst_ref=mine.at[c, d - 1],
            send_sem=asend.at[c], recv_sem=arecv.at[c],
            device_id={"grp": there}, device_id_type=MESH)

    def piece_src(c, q):
        there = close(q)
        row = lax.rem(p + q % n_in, n_in)
        return tiles.at[c, 1, pl.ds(pl.multiple_of(row * hq, 16), hq),
                        pl.ds(pl.multiple_of(there["grp"] * share, 128), share)]

    def spread(c, q):
        return pltpu.make_async_remote_copy(
            src_ref=piece_src(c, q), dst_ref=pieces.at[c, g * n_in + p],
            send_sem=bsend.at[c], recv_sem=brecv.at[c], device_id=close(q), device_id_type=MESH)

    def spread_own(c):
        return pltpu.make_async_copy(piece_src(c, 0), pieces.at[c, g * n_in + p], bown.at[c])

    def replica(c):
        multiply(c, 1)

        def body(q, carry):
            spread(c, q).start()
            return carry

        lax.fori_loop(1, near, body, 0)
        spread_own(c).start()

    def primary(c):
        multiply(c, 0)
        for d in range(1, n_grp):
            swap(c, d).start()

    def add_up(c, ze, extra, store):
        def rows_body(r, carry):
            rows = pl.ds(pl.multiple_of((r % (hq // SUM_ROWS)) * SUM_ROWS, 16), SUM_ROWS)
            lanes = pl.ds(pl.multiple_of((r // (hq // SUM_ROWS)) * 128, 128), 128)

            def add(gd, totals):
                for pk in range(n_in):
                    owner = ownv[gd, z * n_in + pk]
                    piece = pieces[c, gd * n_in + pk, rows, lanes].astype(jnp.float32)
                    piece = piece.reshape(SUM_ROWS // 8, 8, 128)
                    totals = tuple(
                        total + jnp.where((owner == (ze * n_in + b).astype(jnp.float32))[None], piece, 0.0)
                        for b, total in enumerate(totals))
                return totals

            zero = jnp.zeros((SUM_ROWS // 8, 8, 128), jnp.float32)
            totals = lax.fori_loop(0, n_grp, add, (zero,) * n_in)
            for b in range(n_in):
                store(b, rows, lanes, totals[b].reshape(SUM_ROWS, 128))
            return carry

        lax.fori_loop(0, (hq // SUM_ROWS) * (share // 128), rows_body, 0)

    def chain(c, ze, src, dst, way):
        return pltpu.make_async_remote_copy(
            src_ref=zbuf.at[c, src], dst_ref=zbuf.at[c, dst], send_sem=csend.at[c], recv_sem=crecv.at[c, dst],
            device_id={"ep": e + (n_in if way else -n_in)}, device_id_type=MESH)

    def chain_to(ze):
        return jnp.where(ze == z - 1, LINE, ze)

    def pass_on(c, ze):
        edge = (z == 0) | (z == LINE - 1)

        def put(b, rows, lanes, total):
            zbuf[c, ze, b, rows, lanes] = total.astype(jnp.bfloat16)

        def put_add(b, rows, lanes, total):
            total += zbuf[c, ze, b, rows, lanes].astype(jnp.float32)
            zbuf[c, ze, b, rows, lanes] = total.astype(jnp.bfloat16)

        @pl.when(edge)
        def _():
            add_up(c, ze, (), put)

        @pl.when(jnp.logical_not(edge))
        def _():
            chain(c, ze, ze, ze, 0).wait_recv()
            add_up(c, ze, (), put_add)

        @pl.when(ze > z)
        def _():
            chain(c, ze, ze, ze, 1).start()

        @pl.when(ze < z)
        def _():
            chain(c, ze, ze, chain_to(ze), 0).start()

    def sum_first(c):
        wait_bytes(pieces.at[c, pl.ds(0, near - 1)], brecv.at[c])
        spread_own(c).wait()
        for ze in (jnp.where(z < 2, LINE - 1, 0), jnp.where(z < 2, 2, 1)):
            pass_on(c, ze)

    def sum_second(c):
        pass_on(c, z + 1 - 2 * (z % 2))

    def give(c, d):
        there = lax.rem(p + d, n_in)
        return pltpu.make_async_remote_copy(
            src_ref=zbuf.at[c, z, there], dst_ref=back.at[c, p],
            send_sem=dsend.at[c], recv_sem=drecv.at[c],
            device_id={"ep": z * n_in + there}, device_id_type=MESH)

    def sum_last(c):
        def put(slots):
            def store(b, rows, lanes, total):
                for slot in slots:
                    total += zbuf[c, slot, b, rows, lanes].astype(jnp.float32)
                zbuf[c, z, b, rows, lanes] = total.astype(jnp.bfloat16)
            return store

        @pl.when(z > 0)
        def _():
            chain(c, z, z, z, 1).wait_recv()

        @pl.when(z < LINE - 1)
        def _():
            chain(c, z, z, LINE, 0).wait_recv()

        @pl.when(z == 0)
        def _():
            add_up(c, z, (), put((LINE,)))

        @pl.when(z == LINE - 1)
        def _():
            add_up(c, z, (), put((LINE - 1,)))

        @pl.when((z > 0) & (z < LINE - 1))
        def _():
            add_up(c, z, (), put((z, LINE)))

        for d in range(1, n_in):
            give(c, d).start()
        back[c, p] = zbuf[c, z, p]

    def finish(c):
        wait_bytes(mine.at[c], arecv.at[c])
        wait_bytes(back.at[c, pl.ds(0, n_in - 1)], drecv.at[c])
        lanes = pl.ds(pl.multiple_of(c * share, 128), share)

        def body(r, carry):
            rows = pl.ds(pl.multiple_of(r * hq, 16), hq)
            total = tiles[c, 0, rows, share_cols].astype(jnp.float32)
            for d in range(1, n_grp):
                total += mine[c, d - 1, rows, :].astype(jnp.float32)
            out_ref[rows, lanes] = total + back[c, r].astype(jnp.float32)
            return carry

        lax.fori_loop(0, n_in, body, 0)

    def drain(c):
        for i in range(LINE):
            zd = order[i]
            each_hop(lambda way: zcopy(c, zd, way), zd, lambda copy: copy.wait_send())
        wait_bytes(outb.at[c], gsend.at[c])
        wait_bytes(mine.at[c], asend.at[c])
        wait_bytes(pieces.at[c, pl.ds(0, near - 1)], bsend.at[c])
        wait_bytes(zbuf.at[c, pl.ds(0, LINE - 1)], csend.at[c])
        wait_bytes(back.at[c, pl.ds(0, n_in - 1)], dsend.at[c])

    load_meta().wait()
    each_hop(lambda way: mcopy(z, way), z, lambda copy: copy.start())
    for c in range(chunks):
        for part in range(n_grp):
            load(c, part).wait()
        if c < AHEAD:
            own_z(c)
    for d in range(1, n_grp):
        own_copy(d).start()
    build_sel(0)
    for c in range(min(OWN_AHEAD, chunks)):
        pick(c, 0, 1)
    for c in range(min(OWN_AHEAD - 1, chunks)):
        pick(c, 0, 0)

    def at(t, lag, fn):
        @pl.when((t >= lag) & (t < chunks + lag))
        def _():
            fn(t - lag)

    per_step = act_blocks // LINE
    middle = 1 - ends
    END_LAG = max(REP_LAG + 5, PRI_LAG + 2)
    sum_lag = REP_LAG + 1 + middle

    def iteration(t, carry):
        at(t, -AHEAD, own_z)
        for i in range(LINE):
            if i > 0:
                @pl.when(t == 0)
                def _():
                    arrive_meta(i)

                at(t, 0, lambda c: arrive(c, i))

                @pl.when(t == 0)
                def _():
                    build_sel(i)

            at(t, 0 if i else -OWN_AHEAD, lambda c: pick(c, i, 1))
            at(t, PRI_LAG if i else 1 - OWN_AHEAD, lambda c: pick(c, i, 0))

            @pl.when(t < 2)
            def _():
                make_act(t * act_blocks + i * per_step, per_step)

            if i == 0:
                at(t, REP_LAG, replica)
            if i == 1:
                at(t, PRI_LAG + 1, primary)
            if i == 2:
                at(t, sum_lag, sum_first)
            if i == 3:
                at(t, sum_lag + middle, sum_second)
                at(t, REP_LAG + 4, sum_last)
                at(t, END_LAG, finish)
                at(t, END_LAG + 1, drain)

        @pl.when(t == REP_LAG)
        def _():
            for d in range(1, n_grp):
                own_copy(d).wait()

        return carry

    lax.fori_loop(0, chunks + END_LAG + 2, iteration, 0)
    for i in range(LINE):
        zd = order[i]
        each_hop(lambda way: mcopy(zd, way), zd, lambda copy: copy.wait_send())


def run_kernel(owners, meta, out_grad, gate_up, n_ep, n_grp, top):
    tokens, width = out_grad.shape
    cap = gate_up.shape[0] // 2
    hidden = gate_up.shape[1] // 2
    per_src = cap // n_ep
    n_in = n_ep // LINE
    chunks = max(1, min(MAX_CHUNKS, width // n_grp // 128))
    cols = width // chunks
    share = cols // n_grp
    hq = hidden // n_in
    near = n_in * n_grp
    bf16 = jnp.bfloat16
    dma = pltpu.SemaphoreType.DMA
    return pl.pallas_call(
        functools.partial(dispatch_kernel, n_ep, n_grp, per_src, top, chunks),
        out_shape=jax.ShapeDtypeStruct((hidden, width // n_grp), jnp.float32),
        in_specs=[pl.BlockSpec(memory_space=pltpu.SMEM)] + [pl.BlockSpec(memory_space=pl.ANY)] * 3,
        out_specs=pl.BlockSpec(memory_space=pltpu.VMEM),
        scratch_shapes=[
            pltpu.VMEM((chunks, LINE, tokens, cols), bf16),
            pltpu.VMEM((LINE, 2 * top, tokens), jnp.float32),
            pltpu.VMEM((n_grp, n_ep, 8, 128), jnp.float32),
            pltpu.VMEM((LINE, 2, n_in * per_src, tokens), bf16),
            pltpu.VMEM((LINE, 2, n_in * per_src, 128), jnp.float32),
            pltpu.VMEM((chunks, LINE, 2, n_in - 1, per_src, cols), bf16),
            pltpu.VMEM((chunks, 2, cap, cols), bf16),
            pltpu.VMEM((2, hidden, cap), bf16),
            pltpu.VMEM((2, ACT_ROWS, 2 * hidden), bf16),
            pltpu.VMEM((chunks, 2, hidden, cols), bf16),
            pltpu.VMEM((chunks, n_grp - 1, hidden, share), bf16),
            pltpu.VMEM((chunks, near, hq, share), bf16),
            pltpu.VMEM((chunks, LINE + 1, n_in, hq, share), bf16),
            pltpu.VMEM((chunks, n_in, hq, share), bf16),
            dma((chunks + 1, n_grp)),
            dma((2,)),
            dma((n_grp - 1,)),
            dma((n_grp - 1,)),
            dma((2, chunks + 1, LINE)),
            dma((chunks + 1, LINE)),
            dma((chunks,)),
            dma((chunks, 2)),
            dma((chunks,)),
            dma((chunks,)),
            dma((chunks,)),
            dma((chunks,)),
            dma((chunks,)),
            dma((chunks,)),
            dma((chunks, LINE + 1)),
            dma((chunks,)),
            dma((chunks,)),
        ],
        compiler_params=pltpu.CompilerParams(
            collective_id=0, has_side_effects=True, vmem_limit_bytes=67043328),
    )(owners, meta, out_grad, gate_up)


def on_device(out_grad, probs, dest, replica_owner, gate_up):
    n_ep = lax.axis_size("ep")
    n_grp = lax.axis_size("grp")
    top = probs.shape[1]
    cap = gate_up.shape[0] // 2
    hidden = gate_up.shape[1] // 2
    per_src = cap // n_ep
    code = (dest // cap) * per_src + dest % per_src
    code = jnp.where(dest >= 0, code, -1)
    meta = jnp.concatenate([code.T.astype(jnp.float32), probs.T], axis=0)
    total = run_kernel(replica_owner, meta, out_grad, gate_up, n_ep, n_grp, top)
    return total.reshape(1, hidden, -1)


def solution(mesh):
    in_specs = (
        P(("grp", "ep"), None),
        P(("grp", "ep"), None),
        P(("grp", "ep"), None),
        P("grp", None),
        P(("grp", "ep"), None),
    )
    out_specs = P("ep", None, "grp")
    return jax.shard_map(
        on_device, mesh=mesh, in_specs=in_specs, out_specs=out_specs, check_vma=False
    )
```

```python
import functools

import jax
import jax.numpy as jnp
from jax import lax
from jax.experimental import pallas as pl
from jax.experimental.pallas import tpu as pltpu
from jax.sharding import PartitionSpec as P

MESH = pl.DeviceIdType.MESH
LINE = 4
MAX_CHUNKS = 8
ACT_ROWS = 128
AHEAD = 1
REP_LAG = 1
OWN_AHEAD = 4
PRI_LAG = 3
EARLY = 2
REP_TICK = 4
PRIMARY = 23
FIRST_EDGE = 11
FIRST_MID = 15
SECOND_MID = 19
LAST = 23
FINISH = 27
SUM_ROWS = 32


def dispatch_kernel(
    n_ep, n_grp, per_src, top, chunks,
    owners, dest_hbm, prob_hbm, og_hbm, gu_hbm, out_hbm,
    tok, dests, metas, ownv, sel, wgt, outb, inb, act_t, gubuf,
    tiles, mine, pieces, zbuf, back, stage,
    ld_sem, gu_sem, own_send, own_recv, zsend, zrecv, gsend, grecv,
    asend, arecv, bsend, brecv, bown, csend, crecv, dsend, drecv, osem,
):
    n_in = n_ep // LINE
    g = lax.axis_index("grp")
    e = lax.axis_index("ep")
    z = e // n_in
    p = e % n_in
    cols = tok.shape[3]
    share = mine.shape[3]
    tokens = tok.shape[2]
    hidden = act_t.shape[1]
    cap = act_t.shape[2]
    hq = hidden // n_in
    near = n_in * n_grp
    block = 2 * per_src
    share_cols = pl.ds(pl.multiple_of(g * share, 128), share)

    m = ((z + 1) // 2) % 2
    far, rev = (z + 2) % 4, 3 - z
    order = [z, z + 1 - 2 * (z % 2), (1 - m) * far + m * rev, (1 - m) * rev + m * far]

    def wait_bytes(ref, sem):
        pltpu.make_async_copy(ref, ref, sem).wait()

    def load(c, part):
        return pltpu.make_async_copy(
            og_hbm.at[:, pl.ds(pl.multiple_of((part * chunks + c) * share, 128), share)],
            tok.at[c, z, :, pl.ds(part * share, share)], ld_sem.at[c, part])

    def load_dest():
        return pltpu.make_async_copy(dest_hbm, dests, ld_sem.at[chunks, 0])

    def load_prob():
        return pltpu.make_async_copy(prob_hbm, metas.at[z, pl.ds(top, top)], ld_sem.at[chunks, 1])

    def gu_load(q, slot):
        return pltpu.make_async_copy(
            gu_hbm.at[pl.ds(pl.multiple_of(q * ACT_ROWS, ACT_ROWS), ACT_ROWS), :], gubuf.at[slot], gu_sem.at[slot])

    act_blocks = cap // ACT_ROWS

    def gu_block(n):
        return lax.rem(n + act_blocks, 2 * act_blocks)

    load_dest().start()
    load_prob().start()
    for c in range(chunks):
        for part in range(n_grp):
            load(c, part).start()
    gu_load(gu_block(0), 0).start()
    for j in range(n_ep):
        ownv[g, j] = jnp.full((8, 128), owners[0, j], jnp.int32).astype(jnp.float32)

    barrier = pltpu.get_barrier_semaphore()

    def close(q):
        return {"grp": lax.rem(g + q // n_in, n_grp), "ep": z * n_in + lax.rem(p + q % n_in, n_in)}

    def greet(q, carry):
        pl.semaphore_signal(barrier, inc=1, device_id=close(q), device_id_type=MESH)
        return carry

    lax.fori_loop(1, near, greet, 0)

    @pl.when(z > 0)
    def _():
        pl.semaphore_signal(barrier, inc=1, device_id={"ep": e - n_in}, device_id_type=MESH)

    @pl.when(z < LINE - 1)
    def _():
        pl.semaphore_signal(barrier, inc=1, device_id={"ep": e + n_in}, device_id_type=MESH)

    ends = jnp.where(z == 0, 1, 0) + jnp.where(z == LINE - 1, 1, 0)

    def own_copy(d):
        return pltpu.make_async_remote_copy(
            src_ref=ownv.at[g], dst_ref=ownv.at[g], send_sem=own_send.at[d - 1], recv_sem=own_recv.at[d - 1],
            device_id={"grp": lax.rem(g + d, n_grp)}, device_id_type=MESH)

    def zcopy(c, zd, way):
        ref = tok.at[c, zd]
        return pltpu.make_async_remote_copy(
            src_ref=ref, dst_ref=ref, send_sem=zsend.at[way, c, zd], recv_sem=zrecv.at[c, zd],
            device_id={"ep": e + (n_in if way else -n_in)}, device_id_type=MESH)

    def mcopy(zd, way):
        ref = metas.at[zd]
        return pltpu.make_async_remote_copy(
            src_ref=ref, dst_ref=ref, send_sem=zsend.at[way, chunks, zd], recv_sem=zrecv.at[chunks, zd],
            device_id={"ep": e + (n_in if way else -n_in)}, device_id_type=MESH)

    def each_hop(copy, zd, act):
        @pl.when((zd <= z) & (z < LINE - 1))
        def _():
            act(copy(1))

        @pl.when((zd >= z) & (z > 0))
        def _():
            act(copy(0))

    def own_z(c):
        each_hop(lambda way: zcopy(c, z, way), z, lambda copy: copy.start())

    def arrive(c, i):
        zd = order[i]
        zcopy(c, zd, 0).wait_recv()
        each_hop(lambda way: zcopy(c, zd, way), zd, lambda copy: copy.start())

    def arrive_meta(i):
        zd = order[i]
        mcopy(zd, 0).wait_recv()
        each_hop(lambda way: mcopy(zd, way), zd, lambda copy: copy.start())

    def build_sel(i):
        zd = order[i]

        def body(d, carry):
            pp = lax.rem(p + d, n_in)
            for s in range(2):
                first = ((z * n_in + pp) * block + s * per_src).astype(jnp.float32)
                ids = lax.broadcasted_iota(jnp.int32, (per_src, tokens), 0).astype(jnp.float32) + first
                weights = jnp.zeros((per_src, tokens), jnp.float32)
                for k in range(top):
                    code = metas[zd, k:k + 1, :]
                    prob = metas[zd, top + k:top + k + 1, :]
                    weights = jnp.where(ids == code, prob, weights)
                rows = pl.ds(pl.multiple_of(d * per_src, 16), per_src)
                sel[zd, s, rows, :] = jnp.where(weights != 0.0, 1.0, 0.0).astype(jnp.bfloat16)
                wgt[zd, s, rows, :] = jnp.broadcast_to(
                    jnp.sum(weights, axis=1, keepdims=True), (per_src, wgt.shape[3]))
            return carry

        lax.fori_loop(0, n_in, body, 0)

    def gcopy(c, i, s, d):
        src = order[i] * n_in + p
        return pltpu.make_async_remote_copy(
            src_ref=outb.at[c, i, s, d - 1],
            dst_ref=inb.at[c, s, pl.ds(pl.multiple_of(src * per_src, 16), per_src), :],
            send_sem=gsend.at[c], recv_sem=grecv.at[c, s],
            device_id={"ep": z * n_in + lax.rem(p + d, n_in)}, device_id_type=MESH)

    def send_picked(c, i, s):
        for d in range(1, n_in):
            gcopy(c, i, s, d).start()

    def pick(c, i, s, send=True):
        zd = order[i]
        picked = jnp.dot(sel[zd, s], tok[c, zd], preferred_element_type=jnp.float32)
        picked = (picked * jnp.tile(wgt[zd, s], (1, cols // 128))).astype(jnp.bfloat16)
        for d in range(1, n_in):
            outb[c, i, s, d - 1] = picked[d * per_src:(d + 1) * per_src]
            if send:
                gcopy(c, i, s, d).start()
        own = pl.ds(pl.multiple_of((zd * n_in + p) * per_src, 16), per_src)
        inb[c, s, own, :] = picked[:per_src]

    def make_act(first, count):
        def body(n, carry):
            slot = n % 2
            q = gu_block(n)
            gu_load(q, slot).wait()

            @pl.when(n + 1 < 2 * act_blocks)
            def _():
                gu_load(gu_block(n + 1), 1 - slot).start()

            gate = gubuf[slot, :, :hidden].astype(jnp.float32)
            up = gubuf[slot, :, hidden:].astype(jnp.float32)
            half = 0.5 * gate
            act = ((half + half * jnp.tanh(half)) * up).astype(jnp.bfloat16)
            s = q // act_blocks
            r = q % act_blocks
            act_t[s, :, pl.ds(pl.multiple_of(r * ACT_ROWS, ACT_ROWS), ACT_ROWS)] = act.T
            return carry

        lax.fori_loop(first, first + count, body, 0)

    def multiply(c, s):
        wait_bytes(inb.at[c, s, pl.ds(0, (n_ep - LINE) * per_src), :], grecv.at[c, s])
        rows_at = hidden // 2 if cols <= 256 else hidden // 4

        def body(r, carry):
            rows = pl.ds(pl.multiple_of(r * rows_at, 16), rows_at)
            tiles[c, s, rows, :] = jnp.dot(
                act_t[s, rows, :], inb[c, s], preferred_element_type=jnp.float32).astype(jnp.bfloat16)
            return carry

        lax.fori_loop(0, hidden // rows_at, body, 0)

    def swap(c, d):
        there = lax.rem(g + d, n_grp)
        return pltpu.make_async_remote_copy(
            src_ref=tiles.at[c, 0, :, pl.ds(pl.multiple_of(there * share, 128), share)],
            dst_ref=mine.at[c, d - 1],
            send_sem=asend.at[c], recv_sem=arecv.at[c],
            device_id={"grp": there}, device_id_type=MESH)

    def piece_src(c, q):
        there = close(q)
        row = lax.rem(p + q % n_in, n_in)
        return tiles.at[c, 1, pl.ds(pl.multiple_of(row * hq, 16), hq),
                        pl.ds(pl.multiple_of(there["grp"] * share, 128), share)]

    def spread(c, q):
        return pltpu.make_async_remote_copy(
            src_ref=piece_src(c, q), dst_ref=pieces.at[c, g * n_in + p],
            send_sem=bsend.at[c], recv_sem=brecv.at[c], device_id=close(q), device_id_type=MESH)

    def spread_own(c):
        return pltpu.make_async_copy(piece_src(c, 0), pieces.at[c, g * n_in + p], bown.at[c])

    def replica(c):
        multiply(c, 1)

        def body(q, carry):
            spread(c, q).start()
            return carry

        lax.fori_loop(1, near, body, 0)
        spread_own(c).start()

    def primary(c):
        multiply(c, 0)
        for d in range(1, n_grp):
            swap(c, d).start()

    def add_up(c, ze, extra, store):
        def rows_body(r, carry):
            rows = pl.ds(pl.multiple_of((r % (hq // SUM_ROWS)) * SUM_ROWS, 16), SUM_ROWS)
            lanes = pl.ds(pl.multiple_of((r // (hq // SUM_ROWS)) * 128, 128), 128)

            def add(gd, totals):
                for pk in range(n_in):
                    owner = ownv[gd, z * n_in + pk]
                    piece = pieces[c, gd * n_in + pk, rows, lanes].astype(jnp.float32)
                    piece = piece.reshape(SUM_ROWS // 8, 8, 128)
                    totals = tuple(
                        total + jnp.where((owner == (ze * n_in + b).astype(jnp.float32))[None], piece, 0.0)
                        for b, total in enumerate(totals))
                return totals

            zero = jnp.zeros((SUM_ROWS // 8, 8, 128), jnp.float32)
            totals = lax.fori_loop(0, n_grp, add, (zero,) * n_in)
            for b in range(n_in):
                store(b, rows, lanes, totals[b].reshape(SUM_ROWS, 128))
            return carry

        lax.fori_loop(0, (hq // SUM_ROWS) * (share // 128), rows_body, 0)

    def chain(c, ze, src, dst, way):
        return pltpu.make_async_remote_copy(
            src_ref=zbuf.at[c, src], dst_ref=zbuf.at[c, dst], send_sem=csend.at[c], recv_sem=crecv.at[c, dst],
            device_id={"ep": e + (n_in if way else -n_in)}, device_id_type=MESH)

    def chain_to(ze):
        return jnp.where(ze == z - 1, LINE, ze)

    edge = (z == 0) | (z == LINE - 1)
    inner = jnp.logical_not(edge)

    def pass_on(c, ze):
        def put(b, rows, lanes, total):
            zbuf[c, ze, b, rows, lanes] = total.astype(jnp.bfloat16)

        def put_add(b, rows, lanes, total):
            total += zbuf[c, ze, b, rows, lanes].astype(jnp.float32)
            zbuf[c, ze, b, rows, lanes] = total.astype(jnp.bfloat16)

        @pl.when(edge)
        def _():
            add_up(c, ze, (), put)

        @pl.when(inner)
        def _():
            chain(c, ze, ze, ze, 0).wait_recv()
            add_up(c, ze, (), put_add)

        @pl.when(ze > z)
        def _():
            chain(c, ze, ze, ze, 1).start()

        @pl.when(ze < z)
        def _():
            chain(c, ze, ze, chain_to(ze), 0).start()

    def sum_first(c):
        wait_bytes(pieces.at[c, pl.ds(0, near - 1)], brecv.at[c])
        spread_own(c).wait()
        for ze in (jnp.where(z < 2, LINE - 1, 0), jnp.where(z < 2, 2, 1)):
            pass_on(c, ze)

    def sum_second(c):
        pass_on(c, z + 1 - 2 * (z % 2))

    def give(c, d):
        there = lax.rem(p + d, n_in)
        return pltpu.make_async_remote_copy(
            src_ref=zbuf.at[c, z, there], dst_ref=back.at[c, p],
            send_sem=dsend.at[c], recv_sem=drecv.at[c],
            device_id={"ep": z * n_in + there}, device_id_type=MESH)

    def sum_last(c):
        def put(slots):
            def store(b, rows, lanes, total):
                for slot in slots:
                    total += zbuf[c, slot, b, rows, lanes].astype(jnp.float32)
                zbuf[c, z, b, rows, lanes] = total.astype(jnp.bfloat16)
            return store

        @pl.when(z > 0)
        def _():
            chain(c, z, z, z, 1).wait_recv()

        @pl.when(z < LINE - 1)
        def _():
            chain(c, z, z, LINE, 0).wait_recv()

        @pl.when(z == 0)
        def _():
            add_up(c, z, (), put((LINE,)))

        @pl.when(z == LINE - 1)
        def _():
            add_up(c, z, (), put((LINE - 1,)))

        @pl.when((z > 0) & (z < LINE - 1))
        def _():
            add_up(c, z, (), put((z, LINE)))

        for d in range(1, n_in):
            give(c, d).start()
        back[c, p] = zbuf[c, z, p]

    def put_out(c):
        lanes = pl.ds(pl.multiple_of(c * share, 128), share)
        return pltpu.make_async_copy(stage.at[c % 2], out_hbm.at[:, lanes], osem.at[c % 2])

    def finish(c):
        @pl.when(c >= 2)
        def _():
            put_out(c).wait()

        wait_bytes(mine.at[c], arecv.at[c])
        wait_bytes(back.at[c, pl.ds(0, n_in - 1)], drecv.at[c])

        def body(r, carry):
            rows = pl.ds(pl.multiple_of(r * hq, 16), hq)
            total = tiles[c, 0, rows, share_cols].astype(jnp.float32)
            for d in range(1, n_grp):
                total += mine[c, d - 1, rows, :].astype(jnp.float32)
            stage[c % 2, rows, :] = total + back[c, r].astype(jnp.float32)
            return carry

        lax.fori_loop(0, n_in, body, 0)
        put_out(c).start()

    def drain(c):
        for i in range(LINE):
            zd = order[i]
            each_hop(lambda way: zcopy(c, zd, way), zd, lambda copy: copy.wait_send())
        wait_bytes(outb.at[c], gsend.at[c])
        wait_bytes(mine.at[c], asend.at[c])
        wait_bytes(pieces.at[c, pl.ds(0, near - 1)], bsend.at[c])
        wait_bytes(zbuf.at[c, pl.ds(0, LINE - 1)], csend.at[c])
        wait_bytes(back.at[c, pl.ds(0, n_in - 1)], dsend.at[c])

    early = min(EARLY, chunks)
    load_dest().wait()
    rows = dests[...].astype(jnp.float32)
    buffer = jnp.floor((rows + 0.5) * (1.0 / cap))
    place = rows - per_src * jnp.floor((rows + 0.5) * (1.0 / per_src))
    metas[z, :top, :] = buffer * per_src + place
    load_prob().wait()
    build_sel(0)
    for c in range(chunks):
        for part in range(n_grp):
            load(c, part).wait()
        if c < early:
            pick(c, 0, 1, False)
    pl.semaphore_wait(barrier, near - 1 + 2 - ends)
    each_hop(lambda way: mcopy(z, way), z, lambda copy: copy.start())
    for c in range(min(AHEAD, chunks)):
        own_z(c)
    for c in range(early):
        send_picked(c, 0, 1)
    for d in range(1, n_grp):
        own_copy(d).start()
    for c in range(early, min(OWN_AHEAD, chunks)):
        pick(c, 0, 1)
    for c in range(min(OWN_AHEAD - 1, chunks)):
        pick(c, 0, 0)

    def at(t, lag, fn):
        @pl.when((t >= lag) & (t < chunks + lag))
        def _():
            fn(t - lag)

    per_step = act_blocks // LINE
    plan = [
        (LAST, None, sum_last),
        (SECOND_MID, inner, sum_second),
        (FIRST_MID, inner, sum_first),
        (FIRST_EDGE, edge, lambda c: (sum_first(c), sum_second(c))),
        (REP_TICK, None, replica),
        (PRIMARY, None, primary),
        (FINISH, None, finish),
        (FINISH + LINE, None, drain),
    ]

    def iteration(t, carry):
        at(t, -AHEAD, own_z)
        for i in range(LINE):
            if i > 0:
                @pl.when(t == 0)
                def _():
                    arrive_meta(i)

                at(t, 0, lambda c: arrive(c, i))

                @pl.when(t == 0)
                def _():
                    build_sel(i)

            at(t, 0 if i else -OWN_AHEAD, lambda c: pick(c, i, 1))
            at(t, PRI_LAG if i else 1 - OWN_AHEAD, lambda c: pick(c, i, 0))

            @pl.when(t < 2)
            def _():
                make_act(t * act_blocks + i * per_step, per_step)

            for tick, on, fn in plan:
                if tick % LINE == i:
                    if on is None:
                        at(t, tick // LINE, fn)
                    else:
                        @pl.when(on)
                        def _():
                            at(t, tick // LINE, fn)

        @pl.when(t == REP_LAG)
        def _():
            for d in range(1, n_grp):
                own_copy(d).wait()

        return carry

    lax.fori_loop(0, chunks + FINISH // LINE + 1, iteration, 0)
    for i in range(LINE):
        zd = order[i]
        each_hop(lambda way: mcopy(zd, way), zd, lambda copy: copy.wait_send())
    for c in range(max(chunks - 2, 0), chunks):
        put_out(c).wait()


def run_kernel(owners, dest, probs, out_grad, gate_up, n_ep, n_grp, top):
    tokens, width = out_grad.shape
    cap = gate_up.shape[0] // 2
    hidden = gate_up.shape[1] // 2
    per_src = cap // n_ep
    n_in = n_ep // LINE
    chunks = max(1, min(MAX_CHUNKS, width // n_grp // 128))
    cols = width // chunks
    share = cols // n_grp
    hq = hidden // n_in
    near = n_in * n_grp
    bf16 = jnp.bfloat16
    dma = pltpu.SemaphoreType.DMA
    return pl.pallas_call(
        functools.partial(dispatch_kernel, n_ep, n_grp, per_src, top, chunks),
        out_shape=jax.ShapeDtypeStruct((hidden, width // n_grp), jnp.float32),
        in_specs=[pl.BlockSpec(memory_space=pltpu.SMEM)] + [pl.BlockSpec(memory_space=pl.ANY)] * 4,
        out_specs=pl.BlockSpec(memory_space=pl.ANY),
        scratch_shapes=[
            pltpu.VMEM((chunks, LINE, tokens, cols), bf16),
            pltpu.VMEM((top, tokens), jnp.int32),
            pltpu.VMEM((LINE, 2 * top, tokens), jnp.float32),
            pltpu.VMEM((n_grp, n_ep, 8, 128), jnp.float32),
            pltpu.VMEM((LINE, 2, n_in * per_src, tokens), bf16),
            pltpu.VMEM((LINE, 2, n_in * per_src, 128), jnp.float32),
            pltpu.VMEM((chunks, LINE, 2, n_in - 1, per_src, cols), bf16),
            pltpu.VMEM((chunks, 2, cap, cols), bf16),
            pltpu.VMEM((2, hidden, cap), bf16),
            pltpu.VMEM((2, ACT_ROWS, 2 * hidden), bf16),
            pltpu.VMEM((chunks, 2, hidden, cols), bf16),
            pltpu.VMEM((chunks, n_grp - 1, hidden, share), bf16),
            pltpu.VMEM((chunks, near, hq, share), bf16),
            pltpu.VMEM((chunks, LINE + 1, n_in, hq, share), bf16),
            pltpu.VMEM((chunks, n_in, hq, share), bf16),
            pltpu.VMEM((2, hidden, share), jnp.float32),
            dma((chunks + 1, n_grp)),
            dma((2,)),
            dma((n_grp - 1,)),
            dma((n_grp - 1,)),
            dma((2, chunks + 1, LINE)),
            dma((chunks + 1, LINE)),
            dma((chunks,)),
            dma((chunks, 2)),
            dma((chunks,)),
            dma((chunks,)),
            dma((chunks,)),
            dma((chunks,)),
            dma((chunks,)),
            dma((chunks,)),
            dma((chunks, LINE + 1)),
            dma((chunks,)),
            dma((chunks,)),
            dma((2,)),
        ],
        compiler_params=pltpu.CompilerParams(
            collective_id=0, has_side_effects=True, vmem_limit_bytes=67043328),
    )(owners, dest, probs, out_grad, gate_up)


def on_device(out_grad, probs, dest, replica_owner, gate_up):
    n_ep = lax.axis_size("ep")
    n_grp = lax.axis_size("grp")
    top = probs.shape[1]
    hidden = gate_up.shape[1] // 2
    total = run_kernel(replica_owner, dest.T, probs.T, out_grad, gate_up, n_ep, n_grp, top)
    return total.reshape(1, hidden, -1)


def solution(mesh):
    in_specs = (
        P(("grp", "ep"), None),
        P(("grp", "ep"), None),
        P(("grp", "ep"), None),
        P("grp", None),
        P(("grp", "ep"), None),
    )
    out_specs = P("ep", None, "grp")
    return jax.shard_map(
        on_device, mesh=mesh, in_specs=in_specs, out_specs=out_specs, check_vma=False
    )
```

```python
import functools

import jax
import jax.numpy as jnp
from jax import lax
from jax.experimental import pallas as pl
from jax.experimental.pallas import tpu as pltpu
from jax.sharding import PartitionSpec as P

MESH = pl.DeviceIdType.MESH
LINE = 4
MAX_CHUNKS = 8
ACT_ROWS = 128
AHEAD = 1
REP_LAG = 1
OWN_AHEAD = 4
PRI_LAG = 3
EARLY = 2
REP_TICK = 4
PRIMARY = 23
FIRST_EDGE = 10
FIRST_MID = 15
SECOND_MID = 19
LAST = 23
FINISH = 27
SUM_ROWS = 32


def dispatch_kernel(
    n_ep, n_grp, per_src, top, chunks,
    owners, dest_hbm, prob_hbm, og_hbm, gu_hbm, out_hbm,
    tok, dests, metas, ownv, sel, wgt, outb, inb, act_t, gubuf,
    tiles, mine, pieces, zbuf, back, stage,
    ld_sem, gu_sem, own_send, own_recv, zsend, zrecv, gsend, grecv,
    asend, arecv, bsend, brecv, bown, csend, crecv, dsend, drecv, osem,
):
    n_in = n_ep // LINE
    g = lax.axis_index("grp")
    e = lax.axis_index("ep")
    z = e // n_in
    p = e % n_in
    cols = tok.shape[3]
    share = mine.shape[3]
    tokens = tok.shape[2]
    hidden = act_t.shape[1]
    cap = act_t.shape[2]
    hq = hidden // n_in
    near = n_in * n_grp
    block = 2 * per_src
    share_cols = pl.ds(pl.multiple_of(g * share, 128), share)

    m = ((z + 1) // 2) % 2
    far, rev = (z + 2) % 4, 3 - z
    order = [z, z + 1 - 2 * (z % 2), (1 - m) * far + m * rev, (1 - m) * rev + m * far]

    def wait_bytes(ref, sem):
        pltpu.make_async_copy(ref, ref, sem).wait()

    def load(c, part):
        return pltpu.make_async_copy(
            og_hbm.at[:, pl.ds(pl.multiple_of((part * chunks + c) * share, 128), share)],
            tok.at[c, z, :, pl.ds(part * share, share)], ld_sem.at[c, part])

    def load_dest():
        return pltpu.make_async_copy(dest_hbm, dests, ld_sem.at[chunks, 0])

    def load_prob():
        return pltpu.make_async_copy(prob_hbm, metas.at[z, pl.ds(top, top)], ld_sem.at[chunks, 1])

    def gu_load(q, slot):
        return pltpu.make_async_copy(
            gu_hbm.at[pl.ds(pl.multiple_of(q * ACT_ROWS, ACT_ROWS), ACT_ROWS), :], gubuf.at[slot], gu_sem.at[slot])

    act_blocks = cap // ACT_ROWS

    def gu_block(n):
        return lax.rem(n + act_blocks, 2 * act_blocks)

    load_dest().start()
    load_prob().start()
    for c in range(chunks):
        for part in range(n_grp):
            load(c, part).start()
    gu_load(gu_block(0), 0).start()
    for j in range(n_ep):
        ownv[g, j] = jnp.full((8, 128), owners[0, j], jnp.int32).astype(jnp.float32)

    barrier = pltpu.get_barrier_semaphore()

    def close(q):
        return {"grp": lax.rem(g + q // n_in, n_grp), "ep": z * n_in + lax.rem(p + q % n_in, n_in)}

    def greet(q, carry):
        pl.semaphore_signal(barrier, inc=1, device_id=close(q), device_id_type=MESH)
        return carry

    lax.fori_loop(1, near, greet, 0)

    @pl.when(z > 0)
    def _():
        pl.semaphore_signal(barrier, inc=1, device_id={"ep": e - n_in}, device_id_type=MESH)

    @pl.when(z < LINE - 1)
    def _():
        pl.semaphore_signal(barrier, inc=1, device_id={"ep": e + n_in}, device_id_type=MESH)

    ends = jnp.where(z == 0, 1, 0) + jnp.where(z == LINE - 1, 1, 0)

    def own_copy(d):
        return pltpu.make_async_remote_copy(
            src_ref=ownv.at[g], dst_ref=ownv.at[g], send_sem=own_send.at[d - 1], recv_sem=own_recv.at[d - 1],
            device_id={"grp": lax.rem(g + d, n_grp)}, device_id_type=MESH)

    def zcopy(c, zd, way):
        ref = tok.at[c, zd]
        return pltpu.make_async_remote_copy(
            src_ref=ref, dst_ref=ref, send_sem=zsend.at[way, c, zd], recv_sem=zrecv.at[c, zd],
            device_id={"ep": e + (n_in if way else -n_in)}, device_id_type=MESH)

    def mcopy(zd, way):
        ref = metas.at[zd]
        return pltpu.make_async_remote_copy(
            src_ref=ref, dst_ref=ref, send_sem=zsend.at[way, chunks, zd], recv_sem=zrecv.at[chunks, zd],
            device_id={"ep": e + (n_in if way else -n_in)}, device_id_type=MESH)

    def each_hop(copy, zd, act):
        @pl.when((zd <= z) & (z < LINE - 1))
        def _():
            act(copy(1))

        @pl.when((zd >= z) & (z > 0))
        def _():
            act(copy(0))

    def own_z(c):
        each_hop(lambda way: zcopy(c, z, way), z, lambda copy: copy.start())

    def arrive(c, i):
        zd = order[i]
        zcopy(c, zd, 0).wait_recv()
        each_hop(lambda way: zcopy(c, zd, way), zd, lambda copy: copy.start())

    def arrive_meta(i):
        zd = order[i]
        mcopy(zd, 0).wait_recv()
        each_hop(lambda way: mcopy(zd, way), zd, lambda copy: copy.start())

    def build_sel(i):
        zd = order[i]

        def body(d, carry):
            pp = lax.rem(p + d, n_in)
            for s in range(2):
                first = ((z * n_in + pp) * block + s * per_src).astype(jnp.float32)
                ids = lax.broadcasted_iota(jnp.int32, (per_src, tokens), 0).astype(jnp.float32) + first
                weights = jnp.zeros((per_src, tokens), jnp.float32)
                for k in range(top):
                    code = metas[zd, k:k + 1, :]
                    prob = metas[zd, top + k:top + k + 1, :]
                    weights = jnp.where(ids == code, prob, weights)
                rows = pl.ds(pl.multiple_of(d * per_src, 16), per_src)
                sel[zd, s, rows, :] = jnp.where(weights != 0.0, 1.0, 0.0).astype(jnp.bfloat16)
                wgt[zd, s, rows, :] = jnp.broadcast_to(
                    jnp.sum(weights, axis=1, keepdims=True), (per_src, wgt.shape[3]))
            return carry

        lax.fori_loop(0, n_in, body, 0)

    def gcopy(c, i, s, d):
        src = order[i] * n_in + p
        return pltpu.make_async_remote_copy(
            src_ref=outb.at[c, i, s, d - 1],
            dst_ref=inb.at[c, s, pl.ds(pl.multiple_of(src * per_src, 16), per_src), :],
            send_sem=gsend.at[c], recv_sem=grecv.at[c, s],
            device_id={"ep": z * n_in + lax.rem(p + d, n_in)}, device_id_type=MESH)

    def send_picked(c, i, s):
        for d in range(1, n_in):
            gcopy(c, i, s, d).start()

    def pick(c, i, s, send=True):
        zd = order[i]
        picked = jnp.dot(sel[zd, s], tok[c, zd], preferred_element_type=jnp.float32)
        picked = (picked * jnp.tile(wgt[zd, s], (1, cols // 128))).astype(jnp.bfloat16)
        for d in range(1, n_in):
            outb[c, i, s, d - 1] = picked[d * per_src:(d + 1) * per_src]
            if send:
                gcopy(c, i, s, d).start()
        own = pl.ds(pl.multiple_of((zd * n_in + p) * per_src, 16), per_src)
        inb[c, s, own, :] = picked[:per_src]

    def make_act(first, count):
        def body(n, carry):
            slot = n % 2
            q = gu_block(n)
            gu_load(q, slot).wait()

            @pl.when(n + 1 < 2 * act_blocks)
            def _():
                gu_load(gu_block(n + 1), 1 - slot).start()

            gate = gubuf[slot, :, :hidden].astype(jnp.float32)
            up = gubuf[slot, :, hidden:].astype(jnp.float32)
            half = 0.5 * gate
            act = ((half + half * jnp.tanh(half)) * up).astype(jnp.bfloat16)
            s = q // act_blocks
            r = q % act_blocks
            act_t[s, :, pl.ds(pl.multiple_of(r * ACT_ROWS, ACT_ROWS), ACT_ROWS)] = act.T
            return carry

        lax.fori_loop(first, first + count, body, 0)

    def multiply(c, s):
        wait_bytes(inb.at[c, s, pl.ds(0, (n_ep - LINE) * per_src), :], grecv.at[c, s])
        rows_at = hidden // 2 if cols <= 256 else hidden // 4

        def body(r, carry):
            rows = pl.ds(pl.multiple_of(r * rows_at, 16), rows_at)
            tiles[c, s, rows, :] = jnp.dot(
                act_t[s, rows, :], inb[c, s], preferred_element_type=jnp.float32).astype(jnp.bfloat16)
            return carry

        lax.fori_loop(0, hidden // rows_at, body, 0)

    def swap(c, d):
        there = lax.rem(g + d, n_grp)
        return pltpu.make_async_remote_copy(
            src_ref=tiles.at[c, 0, :, pl.ds(pl.multiple_of(there * share, 128), share)],
            dst_ref=mine.at[c, d - 1],
            send_sem=asend.at[c], recv_sem=arecv.at[c],
            device_id={"grp": there}, device_id_type=MESH)

    def piece_src(c, q):
        there = close(q)
        row = lax.rem(p + q % n_in, n_in)
        return tiles.at[c, 1, pl.ds(pl.multiple_of(row * hq, 16), hq),
                        pl.ds(pl.multiple_of(there["grp"] * share, 128), share)]

    def spread(c, q):
        return pltpu.make_async_remote_copy(
            src_ref=piece_src(c, q), dst_ref=pieces.at[c, g * n_in + p],
            send_sem=bsend.at[c], recv_sem=brecv.at[c], device_id=close(q), device_id_type=MESH)

    def spread_own(c):
        return pltpu.make_async_copy(piece_src(c, 0), pieces.at[c, g * n_in + p], bown.at[c])

    def replica(c):
        multiply(c, 1)

        def body(q, carry):
            spread(c, q).start()
            return carry

        lax.fori_loop(1, near, body, 0)
        spread_own(c).start()

    def primary(c):
        multiply(c, 0)
        for d in range(1, n_grp):
            swap(c, d).start()

    def add_up(c, ze, extra, store):
        def rows_body(r, carry):
            rows = pl.ds(pl.multiple_of((r % (hq // SUM_ROWS)) * SUM_ROWS, 16), SUM_ROWS)
            lanes = pl.ds(pl.multiple_of((r // (hq // SUM_ROWS)) * 128, 128), 128)

            def add(gd, totals):
                for pk in range(n_in):
                    owner = ownv[gd, z * n_in + pk]
                    piece = pieces[c, gd * n_in + pk, rows, lanes].astype(jnp.float32)
                    piece = piece.reshape(SUM_ROWS // 8, 8, 128)
                    totals = tuple(
                        total + jnp.where((owner == (ze * n_in + b).astype(jnp.float32))[None], piece, 0.0)
                        for b, total in enumerate(totals))
                return totals

            zero = jnp.zeros((SUM_ROWS // 8, 8, 128), jnp.float32)
            totals = lax.fori_loop(0, n_grp, add, (zero,) * n_in)
            for b in range(n_in):
                store(b, rows, lanes, totals[b].reshape(SUM_ROWS, 128))
            return carry

        lax.fori_loop(0, (hq // SUM_ROWS) * (share // 128), rows_body, 0)

    def chain(c, ze, src, dst, way):
        return pltpu.make_async_remote_copy(
            src_ref=zbuf.at[c, src], dst_ref=zbuf.at[c, dst], send_sem=csend.at[c], recv_sem=crecv.at[c, dst],
            device_id={"ep": e + (n_in if way else -n_in)}, device_id_type=MESH)

    def chain_to(ze):
        return jnp.where(ze == z - 1, LINE, ze)

    edge = (z == 0) | (z == LINE - 1)
    inner = jnp.logical_not(edge)

    def pass_on(c, ze):
        def put(b, rows, lanes, total):
            zbuf[c, ze, b, rows, lanes] = total.astype(jnp.bfloat16)

        def put_add(b, rows, lanes, total):
            total += zbuf[c, ze, b, rows, lanes].astype(jnp.float32)
            zbuf[c, ze, b, rows, lanes] = total.astype(jnp.bfloat16)

        @pl.when(edge)
        def _():
            add_up(c, ze, (), put)

        @pl.when(inner)
        def _():
            chain(c, ze, ze, ze, 0).wait_recv()
            add_up(c, ze, (), put_add)

        @pl.when(ze > z)
        def _():
            chain(c, ze, ze, ze, 1).start()

        @pl.when(ze < z)
        def _():
            chain(c, ze, ze, chain_to(ze), 0).start()

    def sum_first(c):
        wait_bytes(pieces.at[c, pl.ds(0, near - 1)], brecv.at[c])
        spread_own(c).wait()
        for ze in (jnp.where(z < 2, LINE - 1, 0), jnp.where(z < 2, 2, 1)):
            pass_on(c, ze)

    def sum_second(c):
        pass_on(c, z + 1 - 2 * (z % 2))

    def give(c, d):
        there = lax.rem(p + d, n_in)
        return pltpu.make_async_remote_copy(
            src_ref=zbuf.at[c, z, there], dst_ref=back.at[c, p],
            send_sem=dsend.at[c], recv_sem=drecv.at[c],
            device_id={"ep": z * n_in + there}, device_id_type=MESH)

    def sum_last(c):
        def put(slots):
            def store(b, rows, lanes, total):
                for slot in slots:
                    total += zbuf[c, slot, b, rows, lanes].astype(jnp.float32)
                zbuf[c, z, b, rows, lanes] = total.astype(jnp.bfloat16)
            return store

        @pl.when(z > 0)
        def _():
            chain(c, z, z, z, 1).wait_recv()

        @pl.when(z < LINE - 1)
        def _():
            chain(c, z, z, LINE, 0).wait_recv()

        @pl.when(z == 0)
        def _():
            add_up(c, z, (), put((LINE,)))

        @pl.when(z == LINE - 1)
        def _():
            add_up(c, z, (), put((LINE - 1,)))

        @pl.when((z > 0) & (z < LINE - 1))
        def _():
            add_up(c, z, (), put((z, LINE)))

        for d in range(1, n_in):
            give(c, d).start()
        back[c, p] = zbuf[c, z, p]

    def put_out(c):
        lanes = pl.ds(pl.multiple_of(c * share, 128), share)
        return pltpu.make_async_copy(stage.at[c % 2], out_hbm.at[:, lanes], osem.at[c % 2])

    def finish(c):
        @pl.when(c >= 2)
        def _():
            put_out(c).wait()

        wait_bytes(mine.at[c], arecv.at[c])
        wait_bytes(back.at[c, pl.ds(0, n_in - 1)], drecv.at[c])

        def body(r, carry):
            rows = pl.ds(pl.multiple_of(r * hq, 16), hq)
            total = tiles[c, 0, rows, share_cols].astype(jnp.float32)
            for d in range(1, n_grp):
                total += mine[c, d - 1, rows, :].astype(jnp.float32)
            stage[c % 2, rows, :] = total + back[c, r].astype(jnp.float32)
            return carry

        lax.fori_loop(0, n_in, body, 0)
        put_out(c).start()

    def drain(c):
        for i in range(LINE):
            zd = order[i]
            each_hop(lambda way: zcopy(c, zd, way), zd, lambda copy: copy.wait_send())
        wait_bytes(outb.at[c], gsend.at[c])
        wait_bytes(mine.at[c], asend.at[c])
        wait_bytes(pieces.at[c, pl.ds(0, near - 1)], bsend.at[c])
        wait_bytes(zbuf.at[c, pl.ds(0, LINE - 1)], csend.at[c])
        wait_bytes(back.at[c, pl.ds(0, n_in - 1)], dsend.at[c])

    early = min(EARLY, chunks)
    load_dest().wait()
    rows = dests[...].astype(jnp.float32)
    buffer = jnp.floor((rows + 0.5) * (1.0 / cap))
    place = rows - per_src * jnp.floor((rows + 0.5) * (1.0 / per_src))
    metas[z, :top, :] = buffer * per_src + place
    load_prob().wait()
    build_sel(0)
    for c in range(chunks):
        for part in range(n_grp):
            load(c, part).wait()
        if c < early:
            pick(c, 0, 1, False)
    pl.semaphore_wait(barrier, near - 1 + 2 - ends)
    each_hop(lambda way: mcopy(z, way), z, lambda copy: copy.start())
    for c in range(min(AHEAD, chunks)):
        own_z(c)
    for c in range(early):
        send_picked(c, 0, 1)
    for d in range(1, n_grp):
        own_copy(d).start()
    for c in range(early, min(OWN_AHEAD, chunks)):
        pick(c, 0, 1)
    for c in range(min(OWN_AHEAD - 1, chunks)):
        pick(c, 0, 0)

    def at(t, lag, fn):
        @pl.when((t >= lag) & (t < chunks + lag))
        def _():
            fn(t - lag)

    per_step = act_blocks // LINE
    plan = [
        (LAST, None, sum_last),
        (SECOND_MID, inner, sum_second),
        (FIRST_MID, inner, sum_first),
        (FIRST_EDGE, edge, lambda c: (sum_first(c), sum_second(c))),
        (REP_TICK, None, replica),
        (PRIMARY, None, primary),
        (FINISH, None, finish),
        (FINISH + LINE, None, drain),
    ]

    def iteration(t, carry):
        at(t, -AHEAD, own_z)
        for i in range(LINE):
            if i > 0:
                @pl.when(t == 0)
                def _():
                    arrive_meta(i)

                at(t, 0, lambda c: arrive(c, i))

                @pl.when(t == 0)
                def _():
                    build_sel(i)

            at(t, 0 if i else -OWN_AHEAD, lambda c: pick(c, i, 1))
            at(t, PRI_LAG if i else 1 - OWN_AHEAD, lambda c: pick(c, i, 0))

            @pl.when(t < 2)
            def _():
                make_act(t * act_blocks + i * per_step, per_step)

            for tick, on, fn in plan:
                if tick % LINE == i:
                    if on is None:
                        at(t, tick // LINE, fn)
                    else:
                        @pl.when(on)
                        def _():
                            at(t, tick // LINE, fn)

        @pl.when(t == REP_LAG)
        def _():
            for d in range(1, n_grp):
                own_copy(d).wait()

        return carry

    lax.fori_loop(0, chunks + FINISH // LINE + 1, iteration, 0)
    for i in range(LINE):
        zd = order[i]
        each_hop(lambda way: mcopy(zd, way), zd, lambda copy: copy.wait_send())
    for c in range(max(chunks - 2, 0), chunks):
        put_out(c).wait()


def run_kernel(owners, dest, probs, out_grad, gate_up, n_ep, n_grp, top):
    tokens, width = out_grad.shape
    cap = gate_up.shape[0] // 2
    hidden = gate_up.shape[1] // 2
    per_src = cap // n_ep
    n_in = n_ep // LINE
    chunks = max(1, min(MAX_CHUNKS, width // n_grp // 128))
    cols = width // chunks
    share = cols // n_grp
    hq = hidden // n_in
    near = n_in * n_grp
    bf16 = jnp.bfloat16
    dma = pltpu.SemaphoreType.DMA
    return pl.pallas_call(
        functools.partial(dispatch_kernel, n_ep, n_grp, per_src, top, chunks),
        out_shape=jax.ShapeDtypeStruct((hidden, width // n_grp), jnp.float32),
        in_specs=[pl.BlockSpec(memory_space=pltpu.SMEM)] + [pl.BlockSpec(memory_space=pl.ANY)] * 4,
        out_specs=pl.BlockSpec(memory_space=pl.ANY),
        scratch_shapes=[
            pltpu.VMEM((chunks, LINE, tokens, cols), bf16),
            pltpu.VMEM((top, tokens), jnp.int32),
            pltpu.VMEM((LINE, 2 * top, tokens), jnp.float32),
            pltpu.VMEM((n_grp, n_ep, 8, 128), jnp.float32),
            pltpu.VMEM((LINE, 2, n_in * per_src, tokens), bf16),
            pltpu.VMEM((LINE, 2, n_in * per_src, 128), jnp.float32),
            pltpu.VMEM((chunks, LINE, 2, n_in - 1, per_src, cols), bf16),
            pltpu.VMEM((chunks, 2, cap, cols), bf16),
            pltpu.VMEM((2, hidden, cap), bf16),
            pltpu.VMEM((2, ACT_ROWS, 2 * hidden), bf16),
            pltpu.VMEM((chunks, 2, hidden, cols), bf16),
            pltpu.VMEM((chunks, n_grp - 1, hidden, share), bf16),
            pltpu.VMEM((chunks, near, hq, share), bf16),
            pltpu.VMEM((chunks, LINE + 1, n_in, hq, share), bf16),
            pltpu.VMEM((chunks, n_in, hq, share), bf16),
            pltpu.VMEM((2, hidden, share), jnp.float32),
            dma((chunks + 1, n_grp)),
            dma((2,)),
            dma((n_grp - 1,)),
            dma((n_grp - 1,)),
            dma((2, chunks + 1, LINE)),
            dma((chunks + 1, LINE)),
            dma((chunks,)),
            dma((chunks, 2)),
            dma((chunks,)),
            dma((chunks,)),
            dma((chunks,)),
            dma((chunks,)),
            dma((chunks,)),
            dma((chunks,)),
            dma((chunks, LINE + 1)),
            dma((chunks,)),
            dma((chunks,)),
            dma((2,)),
        ],
        compiler_params=pltpu.CompilerParams(
            collective_id=0, has_side_effects=True, vmem_limit_bytes=67043328),
    )(owners, dest, probs, out_grad, gate_up)


def on_device(out_grad, probs, dest, replica_owner, gate_up):
    n_ep = lax.axis_size("ep")
    n_grp = lax.axis_size("grp")
    top = probs.shape[1]
    hidden = gate_up.shape[1] // 2
    total = run_kernel(replica_owner, dest.T, probs.T, out_grad, gate_up, n_ep, n_grp, top)
    return total.reshape(1, hidden, -1)


def solution(mesh):
    in_specs = (
        P(("grp", "ep"), None),
        P(("grp", "ep"), None),
        P(("grp", "ep"), None),
        P("grp", None),
        P(("grp", "ep"), None),
    )
    out_specs = P("ep", None, "grp")
    return jax.shard_map(
        on_device, mesh=mesh, in_specs=in_specs, out_specs=out_specs, check_vma=False
    )
```
